32 devices in a mesh: pw: 16 (over z, x, core), ka: 2 (over y).
Axes of the slice: x: 2, y: 2, z: 4, core: 2. Of those that a mesh axis runs over, the one named last changes fastest.
Arguments:
- waves: bfloat16 [2, 2, 32768, 256], P('ka', None, 'pw'), may hold values from -0.125 to 0.125
- projectors: bfloat16 [2, 2, 32768, 2304], P('ka', None, 'pw'), may hold values from -0.125 to 0.125
- projector_order: int32 [2304], replicated, may hold values from 0 to 2303, each once
- shift_map: int32 [32768], P('pw'), may hold values from 0 to 32767, as said below
- charges: float32 [128, 18, 18], replicated, may hold values from -0.125 to 0.125
- atom_phase: float32 [128], replicated, may hold values from -3.140625 to 3.140625
Outputs:
- margins: float32 [2, 256, 2, 256], P('ka', 'pw')
The draws below stay inside these ranges and needn't reach their ends.
Inputs may be any that keep to these rules, and one draw needn't show every extreme that they name: `projector_order`: each projector slot once. `shift_map`: a permutation of the plane waves that maps every aligned block of 2048 plane waves onto itself.
All inputs are finite; a program needn't handle non-finite values.
Results may differ from the reference program's by a relative error of at most 0.0003.
Values may be sent and summed in bfloat16 or wider, within the bound.
A program may use at most 128 MiB of HBM per device.

```python
import jax
import jax.numpy as jnp
from jax import lax

NB = 256
PPA = 18
PW_DEV = 2048
KPTS = 2
NPW = 32768
ATOMS = 128
NPROJ = 2304


def draw_shift_map(key, part):
    blocks = NPW // PW_DEV
    keys = jax.random.split(key, blocks)
    perms = jax.vmap(lambda single: jax.random.permutation(single, PW_DEV))(keys)
    offsets = (jnp.arange(blocks, dtype=jnp.int32) * PW_DEV)[:, None]
    return (perms.astype(jnp.int32) + offsets).reshape(-1).astype(jnp.int32)


def level_of(rng, extent, shards, low, high):
    def one(position, parts):
        steps = jax.random.uniform(jax.random.fold_in(jax.random.fold_in(rng, 6), position), (parts,), jnp.float32, low / len(shards), high / len(shards))
        return jnp.repeat(jnp.exp(steps), extent[position] // parts).reshape((-1,) + (1,) * (len(extent) - position - 1))

    gain = one(*shards[0])
    for cut in shards[1:]:
        gain = gain * one(*cut)
    return gain


def gaussian(key, dims, width, reach, cuts=(), kind=jnp.bfloat16):
    factor_of = level_of(key, dims, cuts, -0.22, 0.18) if cuts else 1.0
    array = jax.random.normal(key, dims, jnp.float32) * width * factor_of
    return jnp.minimum(jnp.maximum(array, -reach), reach).astype(kind)


def setup_inputs(seed: int = 0) -> dict:
    seeds = jax.random.split(jax.random.key(seed), 7)
    waves = gaussian(seeds[0], (KPTS, 2, NPW, NB), (NPW // 16) ** -0.5, 0.125, ((0, 2), (2, 16)))
    projectors = gaussian(seeds[1], (KPTS, 2, NPW, NPROJ), (NPW // 16) ** -0.5, 0.125, ((0, 2), (2, 16)))
    projector_order = jax.random.permutation(seeds[2], NPROJ).astype(jnp.int32)
    shift_map = draw_shift_map(jax.random.fold_in(seeds[6], 71), 0)
    charges = gaussian(seeds[4], (ATOMS, PPA, PPA), NPROJ ** -0.5, 0.125, (), jnp.float32)
    atom_phase = jnp.clip(jax.random.uniform(seeds[5], (ATOMS,), jnp.float32, -3.140625, 3.140625), -3.140625, 3.140625)
    return {"waves": waves, "projectors": projectors, "projector_order": projector_order, "shift_map": shift_map, "charges": charges, "atom_phase": atom_phase}


def contract(left, right, precision=None):
    return lax.dot_general(left, right, (((0,), (0,)), ((), ())), precision=precision, preferred_element_type=jnp.float32)


def complex_cross(left, right, precision=None):
    real = contract(left[0], right[0], precision) + contract(left[1], right[1], precision)
    imag = contract(left[0], right[1], precision) - contract(left[1], right[0], precision)
    return jnp.stack([real, imag], axis=1)


def reference(waves, projectors, projector_order, shift_map, charges, atom_phase):
    inverse = jnp.argsort(projector_order).astype(jnp.int32)
    sym = 0.5 * (charges + jnp.transpose(charges, (0, 2, 1)))

    def project(pair):
        wave, beta = pair
        real = contract(beta[0], wave[0]) + contract(beta[1], wave[1])
        imag = contract(beta[0], wave[1]) - contract(beta[1], wave[0])
        return jnp.stack([real, imag])[:, inverse, :]

    proj = lax.map(project, (waves, projectors))
    last_wave = waves[0][:, shift_map.astype(jnp.int32), :]
    next_wave = jnp.concatenate([waves[1:], last_wave[None]], axis=0)
    repeated = jnp.repeat(atom_phase, PPA)
    cosine = jnp.cos(repeated)[:, None]
    sine = jnp.sin(repeated)[:, None]
    first = proj[0]
    rotated = jnp.stack([first[0] * cosine + first[1] * sine, first[1] * cosine - first[0] * sine])
    next_proj = jnp.concatenate([proj[1:], rotated[None]], axis=0)

    def margin(items):
        wave, nwave, pk, pn = items
        plane = complex_cross(wave, nwave)
        split = pn.reshape(2, ATOMS, PPA, NB)
        weighted = jnp.einsum("apq,raqj->rapj", sym, split, precision=lax.Precision.HIGHEST).reshape(2, NPROJ, NB)
        aug = complex_cross(pk, weighted, lax.Precision.HIGHEST)
        return plane + aug

    return lax.map(margin, (waves, next_wave, proj, next_proj))
```

```python
import functools

import jax
import jax.numpy as jnp
from jax import lax
from jax.experimental import pallas as pl
from jax.experimental.pallas import tpu as pltpu
from jax.sharding import PartitionSpec as P

PPA = 18
MESH = pl.DeviceIdType.MESH


def from_behind(block, axis, distance):
    devices = range(lax.axis_size(axis))
    route = [((i - distance) % len(devices), i) for i in devices]
    return lax.ppermute(block, axis, route)


def contract(left, right, precision=None):
    return lax.dot_general(
        left,
        right,
        (((0,), (0,)), ((), ())),
        precision=precision,
        preferred_element_type=jnp.float32,
    )


def orders_of(n):
    bits = n.bit_length() - 1
    first = list(range(bits))
    second = [0] + list(range(2, bits)) + [1] if bits > 2 else first
    return first, second


def expand(me, done, free, count):
    index = me & sum(1 << bit for bit in done)
    for place, bit in enumerate(free):
        index = index | (((count >> place) & 1) << bit)
    return index


def halving(n, me, acc, sends, recvs, send_scales, recv_scales, sems):
    orders = orders_of(n)
    bits = len(orders[0])
    rows = acc.shape[2]

    def copies(stream, stage):
        size = n >> (stage + 1)
        base = n - (n >> stage)
        bit = orders[stream][stage]
        partner = me ^ (1 << bit)
        made = []
        for kind, (src, dst) in enumerate(((sends, recvs), (send_scales, recv_scales))):
            made.append(
                pltpu.make_async_remote_copy(
                    src_ref=src.at[stream, pl.ds(base, size)],
                    dst_ref=dst.at[stream, pl.ds(base, size)],
                    send_sem=sems.at[0, stream, stage, kind],
                    recv_sem=sems.at[1, stream, stage, kind],
                    device_id={"pw": partner},
                    device_id_type=MESH,
                )
            )
        return made

    def push(stream, stage):
        size = n >> (stage + 1)
        base = n - (n >> stage)
        bit = orders[stream][stage]
        done = orders[stream][:stage]
        free = [b for b in orders[stream][stage + 1 :]]
        partner = me ^ (1 << bit)

        def code(count, carry):
            chunk = expand(partner, done + [bit], free, count)
            x = acc[stream, chunk]
            top = jnp.max(jnp.abs(x), axis=0, keepdims=True)
            scale = jnp.maximum(top, 1e-30) * (1.0 / 32767.0)
            q = jnp.floor(x * (1.0 / scale) + 0.5)
            sends[stream, base + count] = q.astype(jnp.int32).astype(jnp.int16)
            send_scales[stream, base + count] = scale
            return carry

        lax.fori_loop(0, size, code, 0)
        for copy in copies(stream, stage):
            copy.start()

    def pull(stream, stage):
        size = n >> (stage + 1)
        base = n - (n >> stage)
        bit = orders[stream][stage]
        done = orders[stream][:stage]
        free = [b for b in orders[stream][stage + 1 :]]
        for copy in copies(stream, stage):
            copy.wait()

        def add(count, carry):
            chunk = expand(me, done + [bit], free, count)
            q = recvs[stream, base + count].astype(jnp.int32).astype(jnp.float32)
            acc[stream, chunk] = acc[stream, chunk] + q * recv_scales[stream, base + count]
            return carry

        lax.fori_loop(0, size, add, 0)

    return push, pull, bits


def greet(n, me):
    barrier = pltpu.get_barrier_semaphore()
    bits = n.bit_length() - 1
    for bit in range(bits):
        pl.semaphore_signal(barrier, inc=1, device_id={"pw": me ^ (1 << bit)}, device_id_type=MESH)
    pl.semaphore_wait(barrier, bits)


def scatter_scratch(n, rows, cols):
    bits = n.bit_length() - 1
    return [
        pltpu.VMEM((2, n, rows, cols), jnp.float32),
        pltpu.VMEM((2, n, rows, cols), jnp.int16),
        pltpu.VMEM((2, n, rows, cols), jnp.int16),
        pltpu.VMEM((2, n, 1, cols), jnp.float32),
        pltpu.VMEM((2, n, 1, cols), jnp.float32),
        pltpu.SemaphoreType.DMA((2, 2, bits, 2)),
    ]


def sorted_scatter_kernel(n, inverse, real, imag, out, acc, *rest):
    me = lax.axis_index("pw")
    rows = acc.shape[2]
    greet(n, me)
    push, pull, bits = halving(n, me, acc, *rest)

    def gather(owner_bit, count):
        chunk = ((count << 1) | owner_bit)

        def eight(group, carry):
            for r in range(16):
                row = group * 16 + r
                at = inverse[chunk * rows + row]
                acc[0, chunk, pl.ds(row, 1), :] = real[pl.ds(at, 1), :]
                acc[1, chunk, pl.ds(row, 1), :] = imag[pl.ds(at, 1), :]
            return carry

        lax.fori_loop(0, rows // 16, eight, 0)

    lax.fori_loop(0, n // 2, lambda c, k: (gather(1 - (me & 1), c), k)[1], 0)
    for stream in range(2):
        push(stream, 0)
    lax.fori_loop(0, n // 2, lambda c, k: (gather(me & 1, c), k)[1], 0)
    for stage in range(bits):
        for stream in range(2):
            pull(stream, stage)
            if stage + 1 < bits:
                push(stream, stage + 1)
    out[0] = acc[0, me]
    out[1] = acc[1, me]


def plain_scatter_kernel(n, source, out, acc, *rest):
    me = lax.axis_index("pw")
    greet(n, me)
    push, pull, bits = halving(n, me, acc, *rest)

    def fill(count, carry):
        acc[0, count] = source[0, count]
        acc[1, count] = source[1, count]
        return carry

    lax.fori_loop(0, n, fill, 0)
    for stream in range(2):
        push(stream, 0)
    for stage in range(bits):
        for stream in range(2):
            pull(stream, stage)
            if stage + 1 < bits:
                push(stream, stage + 1)
    out[0] = acc[0, me]
    out[1] = acc[1, me]


def vmem():
    return pl.BlockSpec(memory_space=pltpu.VMEM)


def sorted_scatter(n, inverse, real, imag):
    rows, cols = real.shape[0] // n, real.shape[1]
    return pl.pallas_call(
        functools.partial(sorted_scatter_kernel, n),
        out_shape=jax.ShapeDtypeStruct((2, rows, cols), jnp.float32),
        in_specs=[pl.BlockSpec(memory_space=pltpu.SMEM), vmem(), vmem()],
        out_specs=vmem(),
        scratch_shapes=scatter_scratch(n, rows, cols),
        compiler_params=pltpu.CompilerParams(collective_id=0, has_side_effects=True, vmem_limit_bytes=40 * 2**20),
        cost_estimate=pl.CostEstimate(flops=0, bytes_accessed=60 * 10**6, transcendentals=0),
    )(inverse, real, imag)


def plain_scatter(n, source):
    rows, cols = source.shape[2], source.shape[3]
    return pl.pallas_call(
        functools.partial(plain_scatter_kernel, n),
        out_shape=jax.ShapeDtypeStruct((2, rows, cols), jnp.float32),
        in_specs=[vmem()],
        out_specs=vmem(),
        scratch_shapes=scatter_scratch(n, rows, cols),
        compiler_params=pltpu.CompilerParams(collective_id=1, has_side_effects=True, vmem_limit_bytes=20 * 2**20),
    )(source)


def invert(order, size):
    place = lax.broadcasted_iota(jnp.int32, (size, size), 1)
    slot = lax.broadcasted_iota(jnp.int32, (size, size), 0)
    return jnp.sum(jnp.where(order[None, :] == slot, place, 0), axis=1)


def local(waves, projectors, projector_order, shift_map, charges, atom_phase):
    wave = waves[0]
    beta = projectors[0]
    n = lax.axis_size("pw")
    pw_dev, nb = wave.shape[1], wave.shape[2]
    last_k = lax.axis_index("ka") == lax.axis_size("ka") - 1
    pw_index = lax.axis_index("pw")
    received = from_behind(wave, "ka", -1)
    real = contract(beta[0], wave[0]) + contract(beta[1], wave[1])
    imag = contract(beta[0], wave[1]) - contract(beta[1], wave[0])
    inverse = invert(projector_order, projector_order.shape[0])
    block = sorted_scatter(n, inverse, real, imag)
    next_block = from_behind(block, "ka", -1)
    local_map = shift_map - pw_index * pw_dev
    target = jnp.where(last_k, local_map, jnp.arange(pw_dev, dtype=jnp.int32))
    hot = (target[None, :] == jnp.arange(pw_dev, dtype=jnp.int32)[:, None]).astype(jnp.bfloat16)
    own = lax.dot_general(
        hot, wave, (((1,), (1,)), ((), ())), preferred_element_type=jnp.float32
    ).astype(jnp.bfloat16)
    own_r, own_i = own[:, 0], own[:, 1]
    atom_dev = block.shape[1] // PPA
    phase = lax.dynamic_slice_in_dim(atom_phase, pw_index * atom_dev, atom_dev)
    phase = jnp.where(last_k, phase, 0.0)
    repeated = jnp.repeat(phase, PPA)
    cosine = jnp.cos(repeated)[:, None]
    sine = jnp.sin(repeated)[:, None]
    raw = lax.dynamic_slice_in_dim(charges, pw_index * atom_dev, atom_dev, 0)
    sym = 0.5 * (raw + jnp.transpose(raw, (0, 2, 1)))
    eye = jnp.eye(atom_dev, dtype=jnp.float32)
    full = (sym[:, :, None, :] * eye[:, None, :, None]).reshape(atom_dev * PPA, atom_dev * PPA)
    high = lax.Precision.HIGHEST
    turned = jnp.concatenate(
        [next_block[0] * cosine + next_block[1] * sine, next_block[1] * cosine - next_block[0] * sine], axis=1
    )
    weighted = jnp.dot(full, turned, precision=high, preferred_element_type=jnp.float32)
    wr, wi = weighted[:, :nb], weighted[:, nb:]
    out_r = contract(own_r, received[0]) + contract(own_i, received[1])
    out_i = contract(own_r, received[1]) - contract(own_i, received[0])
    out_r = out_r + contract(block[0], wr, high) + contract(block[1], wi, high)
    out_i = out_i + contract(block[0], wi, high) - contract(block[1], wr, high)
    source = jnp.stack([out_r.reshape(n, nb // n, nb), out_i.reshape(n, nb // n, nb)])
    summed = plain_scatter(n, source)
    return jnp.transpose(summed, (1, 0, 2))[None]


def solution(mesh):
    placed = (P("ka", None, "pw", None), P("ka", None, "pw", None), P(), P("pw"), P(), P())
    return jax.shard_map(
        local, mesh=mesh, in_specs=placed, out_specs=P("ka", "pw", None, None), check_vma=False
    )
```

```python
import functools

import jax
import jax.numpy as jnp
from jax import lax
from jax.experimental import pallas as pl
from jax.experimental.pallas import tpu as pltpu
from jax.sharding import PartitionSpec as P

PPA = 18
MESH = pl.DeviceIdType.MESH


def contract(left, right, precision=None):
    return lax.dot_general(
        left,
        right,
        (((0,), (0,)), ((), ())),
        precision=precision,
        preferred_element_type=jnp.float32,
    )


def orders_of(n):
    bits = n.bit_length() - 1
    first = list(range(bits))
    second = [0] + list(range(2, bits)) + [1] if bits > 2 else first
    return first, second


def expand(me, done, free, count):
    index = me & sum(1 << bit for bit in done)
    for place, bit in enumerate(free):
        index = index | (((count >> place) & 1) << bit)
    return index


def halving(n, me, acc, sends, recvs, send_scales, recv_scales, sems):
    orders = orders_of(n)
    bits = len(orders[0])
    rows = acc.shape[2]

    def copies(stream, stage):
        size = n >> (stage + 1)
        base = n - (n >> stage)
        bit = orders[stream][stage]
        partner = me ^ (1 << bit)
        made = []
        for kind, (src, dst) in enumerate(((sends, recvs), (send_scales, recv_scales))):
            made.append(
                pltpu.make_async_remote_copy(
                    src_ref=src.at[stream, pl.ds(base, size)],
                    dst_ref=dst.at[stream, pl.ds(base, size)],
                    send_sem=sems.at[0, stream, stage, kind],
                    recv_sem=sems.at[1, stream, stage, kind],
                    device_id={"pw": partner},
                    device_id_type=MESH,
                )
            )
        return made

    def push(stream, stage):
        size = n >> (stage + 1)
        base = n - (n >> stage)
        bit = orders[stream][stage]
        done = orders[stream][:stage]
        free = [b for b in orders[stream][stage + 1 :]]
        partner = me ^ (1 << bit)

        def code(count, carry):
            chunk = expand(partner, done + [bit], free, count)
            x = acc[stream, chunk]
            top = jnp.max(jnp.abs(x), axis=0, keepdims=True)
            scale = jnp.maximum(top, 1e-30) * (1.0 / 32767.0)
            q = jnp.floor(x * (1.0 / scale) + 0.5)
            sends[stream, base + count] = q.astype(jnp.int32).astype(jnp.int16)
            send_scales[stream, base + count] = scale
            return carry

        lax.fori_loop(0, size, code, 0)
        for copy in copies(stream, stage):
            copy.start()

    def pull(stream, stage):
        size = n >> (stage + 1)
        base = n - (n >> stage)
        bit = orders[stream][stage]
        done = orders[stream][:stage]
        free = [b for b in orders[stream][stage + 1 :]]
        for copy in copies(stream, stage):
            copy.wait()

        def add(count, carry):
            chunk = expand(me, done + [bit], free, count)
            q = recvs[stream, base + count].astype(jnp.int32).astype(jnp.float32)
            acc[stream, chunk] = acc[stream, chunk] + q * recv_scales[stream, base + count]
            return carry

        lax.fori_loop(0, size, add, 0)

    return push, pull, bits


def fused_kernel(
    n, kn, inverse, target, cosine, sine, sym, wave_hbm, beta_hbm, out,
    wave, beta, rhs, proj, received, own, mine, nextb, kept, local_sems, ka_sems, *scratch
):
    me = lax.axis_index("pw")
    k = lax.axis_index("ka")
    ahead, behind = lax.rem(k + 1, kn), lax.rem(k + kn - 1, kn)
    acc, first = scratch[0], scratch[:6]
    last = scratch[6:]
    acc_last = last[0]
    pw_dev, nb = wave.shape[1], wave.shape[2]
    half = nb // 2
    rows = acc.shape[2]
    tiles = local_sems.shape[0] - 1
    tile = beta.shape[2] // tiles

    def beta_copy(t):
        at = pl.ds(pl.multiple_of(t * tile, tile), tile)
        return pltpu.make_async_copy(beta_hbm.at[0, :, :, at], beta.at[:, :, at], local_sems.at[t + 1])

    own_copy = pltpu.make_async_copy(wave_hbm.at[0], wave, local_sems.at[0])
    own_copy.start()
    for t in range(tiles):
        beta_copy(t).start()

    barrier = pltpu.get_barrier_semaphore()
    bits = n.bit_length() - 1
    for bit in range(bits):
        pl.semaphore_signal(barrier, inc=1, device_id={"pw": me ^ (1 << bit)}, device_id_type=MESH)
    for other in (ahead, behind):
        pl.semaphore_signal(barrier, inc=1, device_id={"ka": other}, device_id_type=MESH)
    pl.semaphore_wait(barrier, bits + 2)

    def ka_copy(src, dst, at):
        return pltpu.make_async_remote_copy(
            src_ref=src,
            dst_ref=dst,
            send_sem=ka_sems.at[0, at],
            recv_sem=ka_sems.at[1, at],
            device_id={"ka": behind},
            device_id_type=MESH,
        )

    wave_copy = ka_copy(wave_hbm.at[0], received, 0)
    wave_copy.start()
    own_copy.wait()
    for stream in range(2):
        cols = slice(stream * half, (stream + 1) * half)
        rhs[stream, 0, :, :half] = wave[0, :, cols]
        rhs[stream, 0, :, half:] = wave[1, :, cols]
        rhs[stream, 1, :, :half] = wave[1, :, cols]
        rhs[stream, 1, :, half:] = -wave[0, :, cols]

    push, pull, bits = halving(n, me, *first)

    def multiply(stream, low, high):
        def step(t, carry):
            if stream == 0:
                beta_copy(t).wait()
            at = pl.ds(pl.multiple_of(t * tile, tile), tile)
            proj[stream, at, :] = contract(beta[0, :, at], rhs[stream, 0]) + contract(beta[1, :, at], rhs[stream, 1])
            return carry

        lax.fori_loop(low, high, step, 0)

    def gather(stream, core):
        def one(count, carry):
            chunk = (count << 1) | core

            def some(group, inner):
                for r in range(16):
                    row = group * 16 + r
                    at = inverse[chunk * rows + row]
                    acc[stream, chunk, pl.ds(row, 1), :] = proj[stream, pl.ds(at, 1), :]
                return inner

            lax.fori_loop(0, rows // 16, some, 0)
            return carry

        lax.fori_loop(0, n // 2, one, 0)

    def permute_own(low, high):
        block = 256 if pw_dev % 256 == 0 else pw_dev

        def step(b, carry):
            at = pl.ds(pl.multiple_of(b * block, block), block)
            slot = lax.broadcasted_iota(jnp.int32, (block, pw_dev), 0) + b * block
            hot = jnp.where(slot == target[...], 1.0, 0.0).astype(jnp.bfloat16)
            for part in range(2):
                own[part, at, :] = jnp.dot(hot, wave[part], preferred_element_type=jnp.float32).astype(jnp.bfloat16)
            return carry

        lax.fori_loop(low * (pw_dev // block) // 2, high * (pw_dev // block) // 2, step, 0)

    multiply(0, 0, tiles)
    gather(0, 1 - (me & 1))
    push(0, 0)
    gather(0, me & 1)
    multiply(1, 0, (tiles + 1) // 2)
    pull(0, 0)
    push(0, 1)
    multiply(1, (tiles + 1) // 2, tiles)
    gather(1, 1 - (me & 1))
    push(1, 0)
    gather(1, me & 1)
    permute_own(0, 1)
    pull(0, 1)
    push(0, 2)
    pull(1, 0)
    push(1, 1)
    permute_own(1, 2)

    def finish(stream):
        mine[stream] = acc[stream, me]
        ka_copy(mine.at[stream], nextb.at[stream], 1 + stream).start()

    for stage in range(2, bits):
        pull(0, stage)
        if stage + 1 < bits:
            push(0, stage + 1)
        else:
            finish(0)
        pull(1, stage - 1)
        push(1, stage)
    wave_copy.wait()
    def plane():
        a, b = received[0], received[1]
        c, d = own[0], own[1]
        kept[0] = contract(c, a) + contract(d, b)
        kept[1] = contract(c, b) - contract(d, a)
    plane()
    pull(1, bits - 1)
    finish(1)
    for stream in range(2):
        ka_copy(mine.at[stream], nextb.at[stream], 1 + stream).wait()
    high = lax.Precision.HIGHEST
    nr = jnp.concatenate([nextb[0, :, :half], nextb[1, :, :half]], axis=1)
    ni = jnp.concatenate([nextb[0, :, half:], nextb[1, :, half:]], axis=1)
    br = jnp.concatenate([mine[0, :, :half], mine[1, :, :half]], axis=1)
    bi = jnp.concatenate([mine[0, :, half:], mine[1, :, half:]], axis=1)
    cos, sin = cosine[...], sine[...]
    charge = sym[...]
    wr = jnp.dot(charge, nr * cos + ni * sin, precision=high, preferred_element_type=jnp.float32)
    wi = jnp.dot(charge, ni * cos - nr * sin, precision=high, preferred_element_type=jnp.float32)
    kept[0] += contract(br, wr, high) + contract(bi, wi, high)
    kept[1] += contract(br, wi, high) - contract(bi, wr, high)
    share = nb // n

    def fill(count, carry):
        at = pl.ds(pl.multiple_of(count * share, share), share)
        acc_last[0, count] = kept[0, at, :]
        acc_last[1, count] = kept[1, at, :]
        return carry

    lax.fori_loop(0, n, fill, 0)
    push, pull, bits = halving(n, me, *last)
    for stream in range(2):
        push(stream, 0)
    for stage in range(bits):
        for stream in range(2):
            pull(stream, stage)
            if stage + 1 < bits:
                push(stream, stage + 1)
    out[0] = acc_last[0, me]
    out[1] = acc_last[1, me]


def scatter_scratch(n, rows, cols):
    bits = n.bit_length() - 1
    return [
        pltpu.VMEM((2, n, rows, cols), jnp.float32),
        pltpu.VMEM((2, n, rows, cols), jnp.int16),
        pltpu.VMEM((2, n, rows, cols), jnp.int16),
        pltpu.VMEM((2, n, 1, cols), jnp.float32),
        pltpu.VMEM((2, n, 1, cols), jnp.float32),
        pltpu.SemaphoreType.DMA((2, 2, bits, 2)),
    ]


def vmem():
    return pl.BlockSpec(memory_space=pltpu.VMEM)


def fused(n, kn, inverse, target, cosine, sine, sym, waves, projectors):
    pw_dev, nb = waves.shape[2], waves.shape[3]
    nproj = projectors.shape[3]
    rows, share = nproj // n, nb // n
    tile = 256 if nproj % 256 == 0 else 128 if nproj % 128 == 0 else nproj
    hbm = pl.BlockSpec(memory_space=pl.ANY)
    return pl.pallas_call(
        functools.partial(fused_kernel, n, kn),
        out_shape=jax.ShapeDtypeStruct((2, share, nb), jnp.float32),
        in_specs=[pl.BlockSpec(memory_space=pltpu.SMEM), vmem(), vmem(), vmem(), vmem(), hbm, hbm],
        out_specs=vmem(),
        scratch_shapes=[
            pltpu.VMEM((2, pw_dev, nb), jnp.bfloat16),
            pltpu.VMEM((2, pw_dev, nproj), jnp.bfloat16),
            pltpu.VMEM((2, 2, pw_dev, nb), jnp.bfloat16),
            pltpu.VMEM((2, nproj, nb), jnp.float32),
            pltpu.VMEM((2, pw_dev, nb), jnp.bfloat16),
            pltpu.VMEM((2, pw_dev, nb), jnp.bfloat16),
            pltpu.VMEM((2, rows, nb), jnp.float32),
            pltpu.VMEM((2, rows, nb), jnp.float32),
            pltpu.VMEM((2, nb, nb), jnp.float32),
            pltpu.SemaphoreType.DMA((nproj // tile + 1,)),
            pltpu.SemaphoreType.DMA((2, 3)),
        ]
        + scatter_scratch(n, rows, nb)
        + scatter_scratch(n, share, nb),
        compiler_params=pltpu.CompilerParams(
            collective_id=0, has_side_effects=True, vmem_limit_bytes=62 * 2**20
        ),
    )(inverse, target, cosine, sine, sym, waves, projectors)


def invert(order, size):
    place = lax.broadcasted_iota(jnp.int32, (size, size), 1)
    slot = lax.broadcasted_iota(jnp.int32, (size, size), 0)
    return jnp.sum(jnp.where(order[None, :] == slot, place, 0), axis=1)


def local(waves, projectors, projector_order, shift_map, charges, atom_phase):
    n = lax.axis_size("pw")
    kn = lax.axis_size("ka")
    pw_dev = waves.shape[2]
    last_k = lax.axis_index("ka") == kn - 1
    pw_index = lax.axis_index("pw")
    inverse = invert(projector_order, projector_order.shape[0])
    local_map = shift_map - pw_index * pw_dev
    target = jnp.where(last_k, local_map, jnp.arange(pw_dev, dtype=jnp.int32))[None, :]
    atom_dev = atom_phase.shape[0] // n
    phase = lax.dynamic_slice_in_dim(atom_phase, pw_index * atom_dev, atom_dev)
    phase = jnp.where(last_k, phase, 0.0)
    repeated = jnp.repeat(phase, PPA)
    cosine = jnp.cos(repeated)[:, None]
    sine = jnp.sin(repeated)[:, None]
    raw = lax.dynamic_slice_in_dim(charges, pw_index * atom_dev, atom_dev, 0)
    sym = 0.5 * (raw + jnp.transpose(raw, (0, 2, 1)))
    eye = jnp.eye(atom_dev, dtype=jnp.float32)
    full = (sym[:, :, None, :] * eye[:, None, :, None]).reshape(atom_dev * PPA, atom_dev * PPA)
    summed = fused(n, kn, inverse, target, cosine, sine, full, waves, projectors)
    return jnp.transpose(summed, (1, 0, 2))[None]


def solution(mesh):
    placed = (P("ka", None, "pw", None), P("ka", None, "pw", None), P(), P("pw"), P(), P())
    return jax.shard_map(
        local, mesh=mesh, in_specs=placed, out_specs=P("ka", "pw", None, None), check_vma=False
    )
```

```python
import functools

import jax
import jax.numpy as jnp
from jax import lax
from jax.experimental import pallas as pl
from jax.experimental.pallas import tpu as pltpu
from jax.sharding import PartitionSpec as P

PPA = 18
MESH = pl.DeviceIdType.MESH


def contract(left, right, precision=None):
    return lax.dot_general(
        left,
        right,
        (((0,), (0,)), ((), ())),
        precision=precision,
        preferred_element_type=jnp.float32,
    )


def orders_of(n):
    bits = n.bit_length() - 1
    first = list(range(bits))
    second = [0] + list(range(2, bits)) + [1] if bits > 2 else first
    return first, second


def expand(me, done, free, count):
    index = me & sum(1 << bit for bit in done)
    for place, bit in enumerate(free):
        index = index | (((count >> place) & 1) << bit)
    return index


def halving(n, me, orders, acc, sends, recvs, send_scales, recv_scales, sems):
    bits = len(orders[0])
    rows = acc.shape[2]

    def copies(stream, stage):
        size = n >> (stage + 1)
        base = n - (n >> stage)
        bit = orders[stream][stage]
        partner = me ^ (1 << bit)
        made = []
        for kind, (src, dst) in enumerate(((sends, recvs), (send_scales, recv_scales))):
            made.append(
                pltpu.make_async_remote_copy(
                    src_ref=src.at[stream, pl.ds(base, size)],
                    dst_ref=dst.at[stream, pl.ds(base, size)],
                    send_sem=sems.at[0, stream, stage, kind],
                    recv_sem=sems.at[1, stream, stage, kind],
                    device_id={"pw": partner},
                    device_id_type=MESH,
                )
            )
        return made

    def push(stream, stage):
        size = n >> (stage + 1)
        base = n - (n >> stage)
        bit = orders[stream][stage]
        done = orders[stream][:stage]
        free = [b for b in orders[stream][stage + 1 :]]
        partner = me ^ (1 << bit)

        def code(count, carry):
            chunk = expand(partner, done + [bit], free, count)
            x = acc[stream, chunk]
            top = jnp.max(jnp.abs(x), axis=0, keepdims=True)
            scale = jnp.maximum(top, 1e-30) * (1.0 / 32767.0)
            q = jnp.floor(x * (1.0 / scale) + 0.5)
            sends[stream, base + count] = q.astype(jnp.int32).astype(jnp.int16)
            send_scales[stream, base + count] = scale
            return carry

        lax.fori_loop(0, size, code, 0)
        for copy in copies(stream, stage):
            copy.start()

    def pull(stream, stage):
        size = n >> (stage + 1)
        base = n - (n >> stage)
        bit = orders[stream][stage]
        done = orders[stream][:stage]
        free = [b for b in orders[stream][stage + 1 :]]
        for copy in copies(stream, stage):
            copy.wait()

        def add(count, carry):
            chunk = expand(me, done + [bit], free, count)
            q = recvs[stream, base + count].astype(jnp.int32).astype(jnp.float32)
            acc[stream, chunk] = acc[stream, chunk] + q * recv_scales[stream, base + count]
            return carry

        lax.fori_loop(0, size, add, 0)

    return push, pull, bits


def fused_kernel(
    n, kn, inverse, shift, cosine, sine, sym, wave_hbm, beta_hbm, out,
    wave, beta, rhs, proj, received, own, mine, nextb, kept, local_sems, ka_sems, *scratch
):
    me = lax.axis_index("pw")
    k = lax.axis_index("ka")
    ahead, behind = lax.rem(k + 1, kn), lax.rem(k + kn - 1, kn)
    acc, first = scratch[0], scratch[:6]
    last = scratch[6:]
    acc_last = last[0]
    pw_dev, nb = wave.shape[1], wave.shape[2]
    half = nb // 2
    rows = acc.shape[2]
    tiles = local_sems.shape[0] - 1
    tile = beta.shape[2] // tiles

    def beta_copy(t):
        at = pl.ds(pl.multiple_of(t * tile, tile), tile)
        return pltpu.make_async_copy(beta_hbm.at[0, :, :, at], beta.at[:, :, at], local_sems.at[t + 1])

    own_copy = pltpu.make_async_copy(wave_hbm.at[0], wave, local_sems.at[0])
    own_copy.start()
    for t in range(tiles):
        beta_copy(t).start()

    barrier = pltpu.get_barrier_semaphore()
    bits = n.bit_length() - 1
    for bit in range(bits):
        pl.semaphore_signal(barrier, inc=1, device_id={"pw": me ^ (1 << bit)}, device_id_type=MESH)
    for other in (ahead, behind):
        pl.semaphore_signal(barrier, inc=1, device_id={"ka": other}, device_id_type=MESH)
    pl.semaphore_wait(barrier, bits + 2)

    def ka_copy(src, dst, at):
        return pltpu.make_async_remote_copy(
            src_ref=src,
            dst_ref=dst,
            send_sem=ka_sems.at[0, at],
            recv_sem=ka_sems.at[1, at],
            device_id={"ka": behind},
            device_id_type=MESH,
        )

    wave_copy = ka_copy(wave_hbm.at[0], received, 0)
    wave_copy.start()
    own_copy.wait()
    for stream in range(2):
        cols = slice(stream * half, (stream + 1) * half)
        rhs[stream, 0, :, :half] = wave[0, :, cols]
        rhs[stream, 0, :, half:] = wave[1, :, cols]
        rhs[stream, 1, :, :half] = wave[1, :, cols]
        rhs[stream, 1, :, half:] = -wave[0, :, cols]

    push, pull, bits = halving(n, me, (orders_of(n)[0],) * 2, *first)

    def multiply(stream, low, high):
        def step(t, carry):
            if stream == 0:
                beta_copy(t).wait()
            at = pl.ds(pl.multiple_of(t * tile, tile), tile)
            proj[stream, at, :] = contract(beta[0, :, at], rhs[stream, 0]) + contract(beta[1, :, at], rhs[stream, 1])
            return carry

        lax.fori_loop(low, high, step, 0)

    unit = 48 if rows % 48 == 0 else 16 if rows % 16 == 0 else 1

    def gather(stream, core):
        def one(count, carry):
            chunk = (count << 1) | core

            def some(group, inner):
                low = pl.multiple_of(group * unit, unit)
                ats = [inverse[chunk * rows + low + r] for r in range(unit)]
                taken = [proj[stream, pl.ds(at, 1), :] for at in ats]
                acc[stream, chunk, pl.ds(low, unit), :] = jnp.concatenate(taken, axis=0)
                return inner

            lax.fori_loop(0, rows // unit, some, 0)
            return carry

        lax.fori_loop(0, n // 2, one, 0)

    every = lax.broadcasted_iota(jnp.int32, (1, pw_dev), 1)
    target = jnp.where(k == kn - 1, shift[...] - me * pw_dev, every)

    def permute_own(low, high):
        block = 256 if pw_dev % 256 == 0 else pw_dev

        def step(b, carry):
            at = pl.ds(pl.multiple_of(b * block, block), block)
            slot = lax.broadcasted_iota(jnp.int32, (block, pw_dev), 0) + b * block
            hot = jnp.where(slot == target, 1.0, 0.0).astype(jnp.bfloat16)
            for part in range(2):
                own[part, at, :] = jnp.dot(hot, wave[part], preferred_element_type=jnp.float32).astype(jnp.bfloat16)
            return carry

        lax.fori_loop(low * (pw_dev // block) // 2, high * (pw_dev // block) // 2, step, 0)

    def finish(stream):
        mine[stream] = acc[stream, me]
        ka_copy(mine.at[stream], nextb.at[stream], 1 + stream).start()

    multiply(0, 0, tiles)
    gather(0, 1 - (me & 1))
    push(0, 0)
    gather(0, me & 1)
    multiply(1, 0, 1)
    pull(0, 0)
    push(0, 1)
    multiply(1, 1, tiles)
    pull(0, 1)
    push(0, 2)
    gather(1, 1 - (me & 1))
    push(1, 0)
    pull(0, 2)
    if bits > 3:
        push(0, 3)
    gather(1, me & 1)
    pull(1, 0)
    push(1, 1)
    for stage in range(3, bits):
        pull(0, stage)
        if stage + 1 < bits:
            push(0, stage + 1)
    finish(0)
    permute_own(0, 2)
    for stage in range(1, bits - 1):
        pull(1, stage)
        push(1, stage + 1)
    wave_copy.wait()
    def plane():
        a, b = received[0], received[1]
        c, d = own[0], own[1]
        kept[0] = contract(c, a) + contract(d, b)
        kept[1] = contract(c, b) - contract(d, a)
    plane()
    pull(1, bits - 1)
    finish(1)
    for stream in range(2):
        ka_copy(mine.at[stream], nextb.at[stream], 1 + stream).wait()
    high = lax.Precision.HIGHEST
    nr = jnp.concatenate([nextb[0, :, :half], nextb[1, :, :half]], axis=1)
    ni = jnp.concatenate([nextb[0, :, half:], nextb[1, :, half:]], axis=1)
    br = jnp.concatenate([mine[0, :, :half], mine[1, :, :half]], axis=1)
    bi = jnp.concatenate([mine[0, :, half:], mine[1, :, half:]], axis=1)
    cos, sin = cosine[...], sine[...]
    charge = sym[...]
    wr = jnp.dot(charge, nr * cos + ni * sin, precision=high, preferred_element_type=jnp.float32)
    wi = jnp.dot(charge, ni * cos - nr * sin, precision=high, preferred_element_type=jnp.float32)
    kept[0] += contract(br, wr, high) + contract(bi, wi, high)
    kept[1] += contract(br, wi, high) - contract(bi, wr, high)
    share = nb // n

    def fill(count, carry):
        at = pl.ds(pl.multiple_of(count * share, share), share)
        acc_last[0, count] = kept[0, at, :]
        acc_last[1, count] = kept[1, at, :]
        return carry

    lax.fori_loop(0, n, fill, 0)
    push, pull, bits = halving(n, me, orders_of(n), *last)
    for stream in range(2):
        push(stream, 0)
    for stage in range(bits):
        for stream in range(2):
            pull(stream, stage)
            if stage + 1 < bits:
                push(stream, stage + 1)
    out[0] = acc_last[0, me]
    out[1] = acc_last[1, me]


def scatter_scratch(n, rows, cols):
    bits = n.bit_length() - 1
    return [
        pltpu.VMEM((2, n, rows, cols), jnp.float32),
        pltpu.VMEM((2, n, rows, cols), jnp.int16),
        pltpu.VMEM((2, n, rows, cols), jnp.int16),
        pltpu.VMEM((2, n, 1, cols), jnp.float32),
        pltpu.VMEM((2, n, 1, cols), jnp.float32),
        pltpu.SemaphoreType.DMA((2, 2, bits, 2)),
    ]


def vmem():
    return pl.BlockSpec(memory_space=pltpu.VMEM)


def fused(n, kn, inverse, target, cosine, sine, sym, waves, projectors):
    pw_dev, nb = waves.shape[2], waves.shape[3]
    nproj = projectors.shape[3]
    rows, share = nproj // n, nb // n
    tile = 256 if nproj % 256 == 0 else 128 if nproj % 128 == 0 else nproj
    hbm = pl.BlockSpec(memory_space=pl.ANY)
    return pl.pallas_call(
        functools.partial(fused_kernel, n, kn),
        out_shape=jax.ShapeDtypeStruct((2, share, nb), jnp.float32),
        in_specs=[pl.BlockSpec(memory_space=pltpu.SMEM), vmem(), vmem(), vmem(), vmem(), hbm, hbm],
        out_specs=vmem(),
        scratch_shapes=[
            pltpu.VMEM((2, pw_dev, nb), jnp.bfloat16),
            pltpu.VMEM((2, pw_dev, nproj), jnp.bfloat16),
            pltpu.VMEM((2, 2, pw_dev, nb), jnp.bfloat16),
            pltpu.VMEM((2, nproj, nb), jnp.float32),
            pltpu.VMEM((2, pw_dev, nb), jnp.bfloat16),
            pltpu.VMEM((2, pw_dev, nb), jnp.bfloat16),
            pltpu.VMEM((2, rows, nb), jnp.float32),
            pltpu.VMEM((2, rows, nb), jnp.float32),
            pltpu.VMEM((2, nb, nb), jnp.float32),
            pltpu.SemaphoreType.DMA((nproj // tile + 1,)),
            pltpu.SemaphoreType.DMA((2, 3)),
        ]
        + scatter_scratch(n, rows, nb)
        + scatter_scratch(n, share, nb),
        compiler_params=pltpu.CompilerParams(
            collective_id=0, has_side_effects=True, vmem_limit_bytes=62 * 2**20
        ),
    )(inverse, target, cosine, sine, sym, waves, projectors)


def invert(order, size):
    place = lax.broadcasted_iota(jnp.int32, (size, size), 1)
    slot = lax.broadcasted_iota(jnp.int32, (size, size), 0)
    return jnp.sum(jnp.where(order[None, :] == slot, place, 0), axis=1)


def local(waves, projectors, projector_order, shift_map, charges, atom_phase):
    n = lax.axis_size("pw")
    kn = lax.axis_size("ka")
    last_k = lax.axis_index("ka") == kn - 1
    pw_index = lax.axis_index("pw")
    inverse = invert(projector_order, projector_order.shape[0])
    atom_dev = atom_phase.shape[0] // n
    phase = lax.dynamic_slice_in_dim(atom_phase, pw_index * atom_dev, atom_dev)
    phase = jnp.where(last_k, phase, 0.0)
    repeated = jnp.repeat(phase, PPA)
    cosine = jnp.cos(repeated)[:, None]
    sine = jnp.sin(repeated)[:, None]
    raw = lax.dynamic_slice_in_dim(charges, pw_index * atom_dev, atom_dev, 0)
    sym = 0.5 * (raw + jnp.transpose(raw, (0, 2, 1)))
    eye = jnp.eye(atom_dev, dtype=jnp.float32)
    full = (sym[:, :, None, :] * eye[:, None, :, None]).reshape(atom_dev * PPA, atom_dev * PPA)
    summed = fused(n, kn, inverse, shift_map[None, :], cosine, sine, full, waves, projectors)
    return jnp.transpose(summed, (1, 0, 2))[None]


def solution(mesh):
    placed = (P("ka", None, "pw", None), P("ka", None, "pw", None), P(), P("pw"), P(), P())
    return jax.shard_map(
        local, mesh=mesh, in_specs=placed, out_specs=P("ka", "pw", None, None), check_vma=False
    )
```
